32 devices in a mesh: groups: 2 (over y), frames: 4 (over z), fsdp: 2 (over x), heads: 2 (over core).
Axes of the slice: x: 2, y: 2, z: 4, core: 2. Of those that a mesh axis runs over, the one named last changes fastest.
Arguments:
- frames_in: bfloat16 [4, 768, 1536], P(('groups', 'fsdp'), 'frames', 'heads'), parts along dimension 0, may hold values from -6 to 6
- lengths: int32 [4], P(('groups', 'fsdp')), parts along dimension 0, may hold values from 192 to 768, as said below
- w_query: bfloat16 [1536, 768], P(('frames', 'fsdp'), 'heads')
- w_key: bfloat16 [1536, 768], P(('frames', 'fsdp'), 'heads'), may hold values from -0.15625 to 0.15625
- w_value: bfloat16 [1536, 768], P(('frames', 'fsdp'), 'heads'), may hold values from -0.15625 to 0.15625
- w_out: bfloat16 [768, 1536], P('heads', ('frames', 'fsdp')), may hold values from -0.21875 to 0.21875
- w_glu: bfloat16 [1536, 2, 1536], P('fsdp', None, 'heads'), may hold values from -0.15625 to 0.15625
- dw_kernel: bfloat16 [31, 1536], P(None, 'heads'), may hold values from -1 to 1
- w_pw: bfloat16 [1536, 1536], P('heads', 'fsdp'), may hold values from -0.15625 to 0.15625
Outputs:
- block_out: bfloat16 [4, 768, 1536], P(('groups', 'fsdp'), 'frames', 'heads'), parts along dimension 0
The draws below stay inside these ranges and needn't reach their ends.
There are 2 independent parts, one for each index of `groups`. The reference program is written for one: setup_inputs(seed, part) draws one part's arguments, and reference() takes and returns one part's arrays. A program takes and returns all parts, laid end to end along the dimension named above; an argument that names none is the same for every part. Nothing has to cross between parts.
Inputs may be any that keep to these rules, and one draw needn't show every extreme that they name: `lengths`: each utterance counts at least 192 valid frames, and in every group some utterance is valid over all 768 frames.
All inputs are finite; a program needn't handle non-finite values.
Results may differ from the reference program's by a relative error of at most 0.012.
The reference program's roundings to bfloat16 on the way (of `normed`, `queries`, `probs`, `context`, `stream`, `normed_two`, `gated` and `hidden`) count: a program that leaves them out, or rounds other values in their place, can miss the bound.
Values may be sent and summed in bfloat16 or wider, within the bound.
No kernel may reach another device: no remote copies, remote signals or barrier semaphores. Data moves between devices by JAX's collectives and lax.ppermute only.
A program may use at most 64 MiB of HBM per device.

```python
import math
import jax
import jax.numpy as jnp
from jax import lax

D = 1536
HEAD_DIM = 96
KERNEL = 31
HEADS = 8
UTTS = 2
LEN = 768
D_ATT = 768


def draw_lengths(key, part):
    drawn = jax.random.randint(key, (UTTS,), LEN // 4, LEN + 1, dtype=jnp.int32)
    chosen = jax.random.randint(jax.random.fold_in(key, 1), (), 0, UTTS, dtype=jnp.int32)
    return jnp.where(jnp.arange(UTTS, dtype=jnp.int32) == chosen, LEN, drawn).astype(jnp.int32)


def draw_w_query(key, part):
    base_scale = 2.0 / math.sqrt(D)
    entries = jnp.clip(jax.random.normal(key, (D, D_ATT), jnp.float32), -6.0, 6.0)
    return (entries * base_scale).astype(jnp.bfloat16)


def shard_levels(rng, dims, split, smallest, top_value):
    def one(axis_at, parts):
        draws = jax.random.uniform(jax.random.fold_in(jax.random.fold_in(rng, 6), axis_at), (parts,), jnp.float32, smallest / len(split), top_value / len(split))
        return jnp.repeat(jnp.exp(draws), dims[axis_at] // parts).reshape((-1,) + (1,) * (len(dims) - axis_at - 1))

    factor_of = one(*split[0])
    for cut in split[1:]:
        factor_of = factor_of * one(*cut)
    return factor_of


def gaussian(own_key, extent, width, bound, cuts=(), kind=jnp.bfloat16):
    values = jax.random.normal(own_key, extent, jnp.float32) * width
    if len(cuts) > 0:
        values = shard_levels(own_key, extent, cuts, -0.22, 0.18) * values
    return jnp.clip(values, min=-bound, max=bound).astype(kind)


def setup_inputs(seed: int = 0, part: int = 0) -> dict:
    seeds = jax.random.split(jax.random.key(seed), 10)
    part_splits = jax.random.split(jax.random.fold_in(seeds[9], part), 10)
    frames_in = gaussian(part_splits[0], (UTTS, LEN, D), 1.0, 6.0, ((0, 2), (1, 4), (2, 2)))
    lengths = draw_lengths(jax.random.fold_in(jax.random.fold_in(seeds[9], part), 71), part)
    w_query = draw_w_query(jax.random.fold_in(seeds[9], 71), part)
    w_key = gaussian(seeds[3], (D, D_ATT), D ** -0.5, 0.15625, ((0, 8), (1, 2)))
    w_value = gaussian(seeds[4], (D, D_ATT), D ** -0.5, 0.15625, ((0, 8), (1, 2)))
    w_out = gaussian(seeds[5], (D_ATT, D), D_ATT ** -0.5, 0.21875, ((0, 2), (1, 8)))
    w_glu = gaussian(seeds[6], (D, 2, D), D ** -0.5, 0.15625, ((0, 2), (2, 2)))
    dw_kernel = gaussian(seeds[7], (KERNEL, D), KERNEL ** -0.5, 1.0, ((1, 2),))
    w_pw = gaussian(seeds[8], (D, D), D ** -0.5, 0.15625, ((0, 2), (1, 2)))
    return {"frames_in": frames_in, "lengths": lengths, "w_query": w_query, "w_key": w_key, "w_value": w_value, "w_out": w_out, "w_glu": w_glu, "dw_kernel": dw_kernel, "w_pw": w_pw}


EPS = 1e-05
NEG_FILL = -1e+30

def layer_norm(rows):
    values = rows.astype(jnp.float32)
    mean_row = lax.optimization_barrier(jnp.mean(values, axis=-1, keepdims=True))
    centred = values - mean_row
    variance = lax.optimization_barrier(jnp.mean(centred * centred, axis=-1, keepdims=True))
    return centred * lax.rsqrt(variance + EPS)

def reference(frames_in, lengths, w_query, w_key, w_value, w_out, w_glu, dw_kernel, w_pw):
    scale_factor = 1.0 / math.sqrt(HEAD_DIM)

    def one_utterance(packed):
        rows, length = packed
        normed = layer_norm(rows).astype(jnp.bfloat16)
        queries = jnp.dot(normed, w_query, preferred_element_type=jnp.float32).astype(jnp.bfloat16)
        key_rows = jnp.dot(normed, w_key, preferred_element_type=jnp.float32).astype(jnp.bfloat16)
        value_rows = jnp.dot(normed, w_value, preferred_element_type=jnp.float32).astype(jnp.bfloat16)
        positions = jnp.arange(LEN, dtype=jnp.int32)
        valid = positions < length

        def one_head(head_args):
            query_head, key_head, value_head = head_args
            scores = jnp.dot(query_head, key_head.T, preferred_element_type=jnp.float32) * scale_factor
            masked = jnp.where(valid[None, :], scores, NEG_FILL)
            row_max = lax.optimization_barrier(jnp.max(masked, axis=1, keepdims=True))
            expo = jnp.where(valid[None, :], jnp.exp(scores - row_max), 0.0)
            denom = lax.optimization_barrier(jnp.sum(expo, axis=1, keepdims=True))
            probs = expo.astype(jnp.bfloat16)
            return jnp.dot(probs, value_head, preferred_element_type=jnp.float32) / denom

        def by_head(matrix):
            return matrix.reshape(LEN, HEADS, HEAD_DIM).transpose(1, 0, 2)
        context = lax.map(one_head, (by_head(queries), by_head(key_rows), by_head(value_rows)))
        context = context.transpose(1, 0, 2).reshape(LEN, D_ATT).astype(jnp.bfloat16)
        stream = (rows.astype(jnp.float32) + jnp.dot(context, w_out, preferred_element_type=jnp.float32)).astype(jnp.bfloat16)
        normed_two = layer_norm(stream).astype(jnp.bfloat16)
        projected = jnp.dot(normed_two, w_glu.reshape(D, 2 * D), preferred_element_type=jnp.float32).reshape(LEN, 2, D)
        gated = projected[:, 0, :] * jax.nn.sigmoid(projected[:, 1, :])
        gated = jnp.where(valid[:, None], gated, 0.0).astype(jnp.bfloat16)
        rim = KERNEL // 2
        padded = jnp.pad(gated.astype(jnp.float32), ((rim, rim), (0, 0)))
        depth = jnp.zeros((LEN, D), jnp.float32)
        for tap_index in range(KERNEL):
            depth = depth + padded[tap_index:tap_index + LEN] * dw_kernel[tap_index].astype(jnp.float32)
        hidden = (depth * jax.nn.sigmoid(depth)).astype(jnp.bfloat16)
        conv_term = jnp.dot(hidden, w_pw, preferred_element_type=jnp.float32)
        return (stream.astype(jnp.float32) + conv_term).astype(jnp.bfloat16)
    return lax.map(one_utterance, (frames_in, lengths))
```

```python
import math

import jax
import jax.numpy as jnp
from jax import lax
from jax.sharding import PartitionSpec as P

HEAD_DIM = 96
KERNEL = 31


EPS = 1e-05
NEG_FILL = -1e30


def padded_2(cells, sides, width):
    for axis, dim in sides:
        count = lax.axis_size(axis)
        ends = count - 1
        head = lax.slice_in_dim(cells, 0, width, axis=dim)
        tail = lax.slice_in_dim(cells, cells.shape[dim] - width, cells.shape[dim], axis=dim)
        cells = jnp.concatenate(
            [
                lax.ppermute(tail, axis, [(i, (i + 1) % count) for i in range(ends)]),
                cells,
                lax.ppermute(head, axis, [((i + 1) % count, i) for i in range(ends)]),
            ],
            axis=dim,
        )
    return cells


def layer_norm(rows):
    values = rows.astype(jnp.float32)
    mean_row = jnp.mean(values, axis=-1, keepdims=True)
    centred = values - mean_row
    variance = jnp.mean(centred * centred, axis=-1, keepdims=True)
    return centred * lax.rsqrt(variance + EPS)


def dot(a, b):
    return jnp.dot(a, b, preferred_element_type=jnp.float32)


def general_shards(frames_in, lengths, w_query, w_key, w_value, w_out, w_glu, dw_kernel, w_pw):
    full_rows = lax.all_gather(frames_in, "heads", axis=2, tiled=True)[0]
    frame_count = full_rows.shape[0]
    half_width = frames_in.shape[2]
    own_start = lax.axis_index("heads") * half_width
    normed = layer_norm(full_rows).astype(jnp.bfloat16)
    att_cols = w_query.shape[1]
    pieces = (
        lax.all_gather(w_query, ("frames", "fsdp"), axis=0, tiled=True),
        lax.all_gather(w_key, ("frames", "fsdp"), axis=0, tiled=True),
        lax.all_gather(w_value, ("frames", "fsdp"), axis=0, tiled=True),
    )
    projected = tuple((dot(normed, piece_part) for piece_part in pieces))
    head_count = att_cols // HEAD_DIM
    queries = projected[0].astype(jnp.bfloat16).reshape(frame_count, head_count, HEAD_DIM)
    key_rows = projected[1].astype(jnp.bfloat16)
    value_rows = projected[2].astype(jnp.bfloat16)
    length = lengths[0]
    scale_factor = 1.0 / math.sqrt(HEAD_DIM)
    pieces = (
        lax.all_gather(key_rows, "frames", axis=0, tiled=True),
        lax.all_gather(value_rows, "frames", axis=0, tiled=True),
    )
    key_block = pieces[0].reshape(-1, head_count, HEAD_DIM)
    value_block = pieces[1].reshape(-1, head_count, HEAD_DIM)
    block_rows = key_block.shape[0]
    scores = (
        jnp.einsum("qhd,khd->qhk", queries, key_block, preferred_element_type=jnp.float32)
        * scale_factor
    )
    valid = jnp.arange(block_rows, dtype=jnp.int32) < length
    masked = jnp.where(valid, scores, NEG_FILL)
    new_max = jnp.max(masked, axis=2)
    expo = jnp.where(valid, jnp.exp(masked - new_max[:, :, None]), 0.0)
    new_sum = jnp.sum(expo, axis=2)
    block_acc = jnp.einsum(
        "qhk,khd->qhd", expo.astype(jnp.bfloat16), value_block, preferred_element_type=jnp.float32
    )
    context = (block_acc / new_sum[:, :, None]).reshape(frame_count, att_cols).astype(jnp.bfloat16)
    partial_value = dot(context, lax.all_gather(w_out, ("frames", "fsdp"), axis=1, tiled=True))
    total = lax.psum(partial_value.astype(jnp.bfloat16), "heads").astype(jnp.float32)
    stream_full = (full_rows.astype(jnp.float32) + total).astype(jnp.bfloat16)
    stream_own = lax.dynamic_slice_in_dim(stream_full, own_start, half_width, 1)
    normed_two = layer_norm(stream_full).astype(jnp.bfloat16)
    channels = w_glu.shape[2]
    glu_pre = jnp.einsum(
        "td,dgc->tgc",
        normed_two,
        lax.all_gather(w_glu, "fsdp", axis=0, tiled=True),
        preferred_element_type=jnp.float32,
    )
    positions = lax.axis_index("frames") * frame_count + jnp.arange(frame_count, dtype=jnp.int32)
    live = positions < length
    gated = jnp.where(
        live[:, None], glu_pre[:, 0, :] * jax.nn.sigmoid(glu_pre[:, 1, :]), 0.0
    ).astype(jnp.bfloat16)
    padded = padded_2(gated, (("frames", 0),), KERNEL // 2)
    depth = jnp.zeros((frame_count, channels), jnp.float32)
    for tap_index in range(KERNEL):
        depth = depth + padded[tap_index : tap_index + frame_count].astype(jnp.float32) * dw_kernel[
            tap_index
        ].astype(jnp.float32)
    hidden = (depth * jax.nn.sigmoid(depth)).astype(jnp.bfloat16)
    conv_part = dot(hidden, lax.all_gather(w_pw, "fsdp", axis=1, tiled=True))
    conv_half = lax.psum_scatter(
        conv_part.astype(jnp.bfloat16), "heads", scatter_dimension=1, tiled=True
    ).astype(jnp.float32)
    result = (stream_own.astype(jnp.float32) + conv_half).astype(jnp.bfloat16)
    return result[None]


def swap(cells, axis, distance=1):
    return lax.ppermute(cells, axis, [(i, i ^ distance) for i in range(lax.axis_size(axis))])


def pick(stacked, index):
    return lax.dynamic_index_in_dim(stacked, index, 0, keepdims=False)


def head_shards(frames_in, lengths, w_query, w_key, w_value, w_out, w_glu, dw_kernel, w_pw):
    blocks = lax.axis_size("frames")
    z = lax.axis_index("frames")
    x = lax.axis_index("fsdp")
    y = lax.axis_index("groups")
    c = lax.axis_index("heads")
    own = frames_in[0]
    rows, half = own.shape
    length = lengths[0]
    rim = 16 * (-(-(KERNEL // 2) // 16))
    wide = rows + 2 * rim

    w_heads = jnp.concatenate(
        [w.reshape(-1, blocks, HEAD_DIM) for w in (w_query, w_key, w_value)], axis=2
    )
    w_heads = w_heads.transpose(1, 0, 2)
    with jax.named_scope("qkv_z"):
        w_mine = [pick(w_heads, z)] + [
            swap(pick(w_heads, z ^ k), "frames", k) for k in range(1, blocks)
        ]
    with jax.named_scope("qkv_x"):
        w_other = [swap(w, "fsdp") for w in w_mine]

    with jax.named_scope("frames_z"):
        far = swap(own, "frames", 3)
        near = swap(own, "frames", 1)
        relayed = swap(far, "frames", 1)
    owns = (own, near, relayed, far)
    with jax.named_scope("frames_c"):
        others = [swap(t, "heads") for t in owns]

    with jax.named_scope("out_x"):
        out_other = swap(w_out, "fsdp")
    out_block = jnp.where(
        x == 0,
        jnp.concatenate([w_out, out_other], axis=1),
        jnp.concatenate([out_other, w_out], axis=1),
    )
    out_rows = out_block.shape[0] // 2
    out_half = lax.dynamic_slice_in_dim(out_block, y * out_rows, out_rows, 0)
    with jax.named_scope("out_z"):
        out_far = swap(out_half, "frames", 3)
        out_near = swap(out_half, "frames", 1)
        out_relayed = swap(out_far, "frames", 1)
    out_halves = (out_half, out_near, out_relayed, out_far)
    with jax.named_scope("out_y"):
        out_halves_two = [swap(t, "groups") for t in out_halves]

    glu_own = jnp.concatenate([w_glu[:, 0, :], w_glu[:, 1, :]], axis=1)
    parts = 2
    glu_rows = glu_own.shape[0] // 2
    glu_send = lax.dynamic_slice_in_dim(glu_own, y * glu_rows, glu_rows, 0)
    with jax.named_scope("glu_x"):
        glu_a = [swap(t, "fsdp") for t in jnp.split(glu_send, parts, axis=0)]
    with jax.named_scope("glu_y"):
        glu_b = [swap(t, "groups") for t in glu_a]
    pw_rows = w_pw.shape[0] // 2
    pw_send = lax.dynamic_slice_in_dim(w_pw, y * pw_rows, pw_rows, 0)
    with jax.named_scope("pw_x"):
        pw_a = swap(pw_send, "fsdp")
    with jax.named_scope("pw_y"):
        pw_b = swap(pw_a, "groups")

    both = [jnp.concatenate([a, b], axis=1) for a, b in zip(owns, others)]
    stacked = jnp.stack(both)
    full_rows = jnp.concatenate([pick(stacked, z ^ j) for j in range(blocks)], axis=0)
    normed = layer_norm(full_rows).astype(jnp.bfloat16)
    w_stack = jnp.stack(
        [
            jnp.where(x == 0, jnp.concatenate([a, b], axis=0), jnp.concatenate([b, a], axis=0))
            for a, b in zip(w_mine, w_other)
        ]
    )
    w_full = jnp.concatenate([pick(w_stack, z ^ j ^ (2 * c)) for j in range(blocks)], axis=0)
    projected = dot(normed, w_full).astype(jnp.bfloat16)
    queries = projected[:, :HEAD_DIM]
    keys = projected[:, HEAD_DIM : 2 * HEAD_DIM]
    values = projected[:, 2 * HEAD_DIM :]
    scores = lax.dot_general(
        queries, keys, (((1,), (1,)), ((), ())), preferred_element_type=jnp.float32
    ) * (1.0 / math.sqrt(HEAD_DIM))
    valid = jnp.arange(blocks * rows, dtype=jnp.int32) < length
    row_max = jnp.max(jnp.where(valid, scores, NEG_FILL), axis=1, keepdims=True)
    expo = jnp.where(valid, jnp.exp(jnp.where(valid, scores, NEG_FILL) - row_max), 0.0)
    denom = jnp.sum(expo, axis=1, keepdims=True)
    context = (dot(expo.astype(jnp.bfloat16), values) / denom).astype(jnp.bfloat16)

    padded_context = jnp.pad(context, ((rim, rim), (0, 0)))
    windows = [
        lax.dynamic_slice_in_dim(padded_context, (z ^ k) * rows, wide, 0) for k in range(blocks)
    ]
    with jax.named_scope("ctx_z"):
        heads_in = [windows[0]] + [swap(windows[k], "frames", k) for k in range(1, blocks)]
    heads_stack = jnp.stack(heads_in)
    head_rows = jnp.concatenate(
        [pick(heads_stack, z ^ j ^ (2 * y)) for j in range(blocks)], axis=1
    )
    out_stack = jnp.stack(
        [jnp.concatenate([a, b], axis=0) for a, b in zip(out_halves, out_halves_two)]
    )
    out_full = jnp.concatenate(
        [pick(out_stack, z ^ j ^ (2 * c)) for j in range(blocks)], axis=1
    )
    partial_value = dot(head_rows, out_full).astype(jnp.bfloat16)
    with jax.named_scope("partial_c"):
        partial_other = swap(partial_value, "heads")
    total = partial_value.astype(jnp.float32) + jnp.concatenate(
        [partial_other[:, half:], partial_other[:, :half]], axis=1
    ).astype(jnp.float32)
    window_rows = lax.dynamic_slice_in_dim(
        jnp.pad(full_rows, ((rim, rim), (0, 0))), z * rows, wide, 0
    )
    stream = (window_rows.astype(jnp.float32) + total).astype(jnp.bfloat16)
    normed_two = layer_norm(stream).astype(jnp.bfloat16)

    same = x == c
    normed_own = jnp.where(same, normed_two[:, :half], normed_two[:, half:])
    normed_other = jnp.where(same, normed_two[:, half:], normed_two[:, :half])
    slices = [
        lax.dynamic_slice_in_dim(normed_other, start * glu_rows, glu_rows, 1) for start in (y, 1 - y)
    ]
    pre = dot(normed_own, glu_own)
    for cols, pieces in zip(slices, (glu_a, glu_b)):
        pre = pre + dot(cols, jnp.concatenate(pieces, axis=0))
    channels = w_glu.shape[2]
    positions = z * rows - rim + jnp.arange(wide, dtype=jnp.int32)
    live = (positions >= 0) & (positions < length)
    gated = jnp.where(
        live[:, None], pre[:, :channels] * jax.nn.sigmoid(pre[:, channels:]), 0.0
    ).astype(jnp.bfloat16)
    depth = jnp.zeros((rows, channels), jnp.float32)
    first = rim - KERNEL // 2
    for tap in range(KERNEL):
        depth = depth + gated[first + tap : first + tap + rows].astype(jnp.float32) * dw_kernel[
            tap
        ].astype(jnp.float32)
    hidden = (depth * jax.nn.sigmoid(depth)).astype(jnp.bfloat16)

    part_own = dot(hidden, w_pw)
    part_other = dot(
        lax.dynamic_slice_in_dim(hidden, y * pw_rows, pw_rows, 1), pw_a
    ) + dot(lax.dynamic_slice_in_dim(hidden, (1 - y) * pw_rows, pw_rows, 1), pw_b)
    keep = jnp.where(same, part_own, part_other).astype(jnp.bfloat16)
    send = jnp.where(same, part_other, part_own).astype(jnp.bfloat16)
    with jax.named_scope("conv_c"):
        arrived = swap(send, "heads")
    conv = keep.astype(jnp.float32) + arrived.astype(jnp.float32)
    result = stream[rim : rim + rows, :half].astype(jnp.float32) + conv
    return result.astype(jnp.bfloat16)[None]


def solution(mesh):
    in_specs = (
        P(("groups", "fsdp"), "frames", "heads"),
        P(("groups", "fsdp")),
        P(("frames", "fsdp"), "heads"),
        P(("frames", "fsdp"), "heads"),
        P(("frames", "fsdp"), "heads"),
        P("heads", ("frames", "fsdp")),
        P("fsdp", None, "heads"),
        P(None, "heads"),
        P("heads", "fsdp"),
    )
    out_specs = P(("groups", "fsdp"), "frames", "heads")
    sizes = mesh.shape

    def shards(*args):
        head_count = args[2].shape[1] // HEAD_DIM
        by_head = (
            head_count == sizes["frames"] == 4
            and sizes["fsdp"] == sizes["groups"] == sizes["heads"] == 2
        )
        return (head_shards if by_head else general_shards)(*args)

    return jax.shard_map(shards, mesh=mesh, in_specs=in_specs, out_specs=out_specs, check_vma=False)
```

```python
import functools
import math

import jax
import jax.numpy as jnp
from jax import lax
from jax.experimental import pallas as pl
from jax.experimental.pallas import tpu as pltpu
from jax.sharding import PartitionSpec as P


HEAD_DIM = 96
KERNEL = 31


EPS = 1e-05
NEG_FILL = -1e30


def padded_2(cells, sides, width):
    for axis, dim in sides:
        count = lax.axis_size(axis)
        ends = count - 1
        head = lax.slice_in_dim(cells, 0, width, axis=dim)
        tail = lax.slice_in_dim(cells, cells.shape[dim] - width, cells.shape[dim], axis=dim)
        cells = jnp.concatenate(
            [
                lax.ppermute(tail, axis, [(i, (i + 1) % count) for i in range(ends)]),
                cells,
                lax.ppermute(head, axis, [((i + 1) % count, i) for i in range(ends)]),
            ],
            axis=dim,
        )
    return cells


def layer_norm(rows):
    values = rows.astype(jnp.float32)
    mean_row = jnp.mean(values, axis=-1, keepdims=True)
    centred = values - mean_row
    variance = jnp.mean(centred * centred, axis=-1, keepdims=True)
    return centred * lax.rsqrt(variance + EPS)


def dot(a, b):
    return jnp.dot(a, b, preferred_element_type=jnp.float32)


def general_shards(frames_in, lengths, w_query, w_key, w_value, w_out, w_glu, dw_kernel, w_pw):
    full_rows = lax.all_gather(frames_in, "heads", axis=2, tiled=True)[0]
    frame_count = full_rows.shape[0]
    half_width = frames_in.shape[2]
    own_start = lax.axis_index("heads") * half_width
    normed = layer_norm(full_rows).astype(jnp.bfloat16)
    att_cols = w_query.shape[1]
    pieces = (
        lax.all_gather(w_query, ("frames", "fsdp"), axis=0, tiled=True),
        lax.all_gather(w_key, ("frames", "fsdp"), axis=0, tiled=True),
        lax.all_gather(w_value, ("frames", "fsdp"), axis=0, tiled=True),
    )
    projected = tuple((dot(normed, piece_part) for piece_part in pieces))
    head_count = att_cols // HEAD_DIM
    queries = projected[0].astype(jnp.bfloat16).reshape(frame_count, head_count, HEAD_DIM)
    key_rows = projected[1].astype(jnp.bfloat16)
    value_rows = projected[2].astype(jnp.bfloat16)
    length = lengths[0]
    scale_factor = 1.0 / math.sqrt(HEAD_DIM)
    pieces = (
        lax.all_gather(key_rows, "frames", axis=0, tiled=True),
        lax.all_gather(value_rows, "frames", axis=0, tiled=True),
    )
    key_block = pieces[0].reshape(-1, head_count, HEAD_DIM)
    value_block = pieces[1].reshape(-1, head_count, HEAD_DIM)
    block_rows = key_block.shape[0]
    scores = (
        jnp.einsum("qhd,khd->qhk", queries, key_block, preferred_element_type=jnp.float32)
        * scale_factor
    )
    valid = jnp.arange(block_rows, dtype=jnp.int32) < length
    masked = jnp.where(valid, scores, NEG_FILL)
    new_max = jnp.max(masked, axis=2)
    expo = jnp.where(valid, jnp.exp(masked - new_max[:, :, None]), 0.0)
    new_sum = jnp.sum(expo, axis=2)
    block_acc = jnp.einsum(
        "qhk,khd->qhd", expo.astype(jnp.bfloat16), value_block, preferred_element_type=jnp.float32
    )
    context = (block_acc / new_sum[:, :, None]).reshape(frame_count, att_cols).astype(jnp.bfloat16)
    partial_value = dot(context, lax.all_gather(w_out, ("frames", "fsdp"), axis=1, tiled=True))
    total = lax.psum(partial_value.astype(jnp.bfloat16), "heads").astype(jnp.float32)
    stream_full = (full_rows.astype(jnp.float32) + total).astype(jnp.bfloat16)
    stream_own = lax.dynamic_slice_in_dim(stream_full, own_start, half_width, 1)
    normed_two = layer_norm(stream_full).astype(jnp.bfloat16)
    channels = w_glu.shape[2]
    glu_pre = jnp.einsum(
        "td,dgc->tgc",
        normed_two,
        lax.all_gather(w_glu, "fsdp", axis=0, tiled=True),
        preferred_element_type=jnp.float32,
    )
    positions = lax.axis_index("frames") * frame_count + jnp.arange(frame_count, dtype=jnp.int32)
    live = positions < length
    gated = jnp.where(
        live[:, None], glu_pre[:, 0, :] * jax.nn.sigmoid(glu_pre[:, 1, :]), 0.0
    ).astype(jnp.bfloat16)
    padded = padded_2(gated, (("frames", 0),), KERNEL // 2)
    depth = jnp.zeros((frame_count, channels), jnp.float32)
    for tap_index in range(KERNEL):
        depth = depth + padded[tap_index : tap_index + frame_count].astype(jnp.float32) * dw_kernel[
            tap_index
        ].astype(jnp.float32)
    hidden = (depth * jax.nn.sigmoid(depth)).astype(jnp.bfloat16)
    conv_part = dot(hidden, lax.all_gather(w_pw, "fsdp", axis=1, tiled=True))
    conv_half = lax.psum_scatter(
        conv_part.astype(jnp.bfloat16), "heads", scatter_dimension=1, tiled=True
    ).astype(jnp.float32)
    result = (stream_own.astype(jnp.float32) + conv_half).astype(jnp.bfloat16)
    return result[None]


def swap(cells, axis, distance=1):
    return lax.ppermute(cells, axis, [(i, i ^ distance) for i in range(lax.axis_size(axis))])


def local(kernel, out_shape, args, scratch=(), flops=0, in_place=()):
    out_bytes = sum(math.prod(s.shape) * s.dtype.itemsize for s in jax.tree.leaves(out_shape))
    in_bytes = sum(math.prod(a.shape) * a.dtype.itemsize for a in args)
    vmem = pl.BlockSpec(memory_space=pltpu.VMEM)
    in_specs = [
        pl.BlockSpec(memory_space=pltpu.SMEM)
        if i == 0
        else pl.BlockSpec(memory_space=pl.ANY)
        if i in in_place
        else vmem
        for i in range(len(args))
    ]
    return pl.pallas_call(
        kernel,
        out_shape=out_shape,
        in_specs=in_specs,
        out_specs=jax.tree.map(lambda _: vmem, out_shape),
        scratch_shapes=list(scratch),
        cost_estimate=pl.CostEstimate(
            flops=flops, bytes_accessed=in_bytes + out_bytes, transcendentals=0
        ),
    )(*args)


def pack_kernel(pos, w_query, w_key, w_value, *outs):
    count = len(outs)
    groups = outs[0].shape[1] // (3 * HEAD_DIM)
    size = outs[0].shape[0]
    for here in range(count):

        @pl.when(pos[0] == here)
        def _():
            for k, out in enumerate(outs):
                first = (here ^ k) * HEAD_DIM
                for part, w in enumerate((w_query, w_key, w_value)):
                    for g in range(groups):
                        at = (3 * g + part) * HEAD_DIM
                        out[:, at : at + HEAD_DIM] = w[
                            g * size : (g + 1) * size, first : first + HEAD_DIM
                        ]


def normalised(parts):
    values = [p.astype(jnp.float32) for p in parts]
    width = sum(v.shape[1] for v in values)
    mean_row = sum(jnp.sum(v, axis=1, keepdims=True) for v in values) / width
    centred = [v - mean_row for v in values]
    variance = sum(jnp.sum(v * v, axis=1, keepdims=True) for v in centred) / width
    scale = lax.rsqrt(variance + EPS)
    return [(v * scale).astype(jnp.bfloat16) for v in centred]


def projected(pos, own, other, weights):
    half = own.shape[1]
    total = 0.0
    for flip, rows in enumerate(normalised((own[...], other[...]))):
        at = pl.multiple_of((pos[3] ^ flip) * half, 128)
        total = total + dot(rows, weights[pl.ds(at, half), :])
    return total.astype(jnp.bfloat16)


def early_kernel(count, pos, *refs):
    packs, refs = refs[: 2 * count], refs[2 * count :]
    outs, refs = refs[-3:], refs[:-3]
    weights, three, window = outs
    size, lanes = packs[0].shape
    groups = lanes // weights.shape[1]
    for k in range(count):
        for other in range(2):
            shard = 2 * (pos[0] ^ k) + (pos[1] ^ other)
            for g in range(groups):
                rows = pl.ds(pl.multiple_of(shard * (groups * size) + g * size, 16), size)
                cols = slice(g * weights.shape[1], (g + 1) * weights.shape[1])
                weights[rows, :] = packs[other * count + k][:, cols]
    blocks = list(zip(refs[::2], refs[1::2]))
    for i, (own, other) in enumerate(blocks):
        three[i] = projected(pos, own, other, weights)
    rows, half = blocks[0][0].shape
    rim = (window.shape[0] - rows) // 2
    odd = pos[0] % 2 == 1
    for flip in range(2):
        cols = pl.ds(pl.multiple_of((pos[3] ^ flip) * half, 128), half)
        mine, near, far = (pair[flip] for pair in blocks)
        window[rim : rim + rows, cols] = mine[...]
        window[:rim, cols] = jnp.where(odd, near[rows - rim :, :], far[rows - rim :, :])
        window[rim + rows :, cols] = jnp.where(odd, far[:rim, :], near[:rim, :])


def attend_kernel(pos, own, other, weights, three, *refs):
    outs, (joined, context) = refs[:-2], refs[-2:]
    count = len(outs)
    rows = own.shape[0]
    rim = (outs[0].shape[0] - rows) // 2
    for k, i in ((0, 0), (1, 1), (3, 2)):
        joined[pl.ds(pl.multiple_of((pos[0] ^ k) * rows, 16), rows), :] = three[i]
    at = pl.multiple_of((pos[0] ^ 2) * rows, 16)
    joined[pl.ds(at, rows), :] = projected(pos, own, other, weights)
    keys = joined[:, HEAD_DIM : 2 * HEAD_DIM]
    values = joined[:, 2 * HEAD_DIM :]
    valid = lax.broadcasted_iota(jnp.int32, (rows, count * rows), 1) < pos[4]
    context[:rim, :] = jnp.zeros((rim, HEAD_DIM), jnp.bfloat16)
    context[rim + count * rows :, :] = jnp.zeros((rim, HEAD_DIM), jnp.bfloat16)
    for b in range(count):
        scores = lax.dot_general(
            joined[b * rows : (b + 1) * rows, :HEAD_DIM],
            keys,
            (((1,), (1,)), ((), ())),
            preferred_element_type=jnp.float32,
        ) * (1.0 / math.sqrt(HEAD_DIM))
        masked = jnp.where(valid, scores, NEG_FILL)
        row_max = jnp.max(masked, axis=1, keepdims=True)
        expo = jnp.where(valid, jnp.exp(masked - row_max), 0.0)
        denom = jnp.sum(expo, axis=1, keepdims=True)
        mixed = dot(expo.astype(jnp.bfloat16), values) / denom
        context[rim + b * rows : rim + (b + 1) * rows, :] = mixed.astype(jnp.bfloat16)
    for k, out in enumerate(outs):
        at = pl.multiple_of((pos[0] ^ k) * rows, 16)
        out[...] = context[pl.ds(at, rows + 2 * rim), :]


def out_kernel(pos, *refs):
    count = (len(refs) - 3) // 3
    pieces, first, second = refs[:count], refs[count : 2 * count], refs[2 * count : 3 * count]
    out, by_head, weights = refs[-3:]
    for k, piece in enumerate(pieces):
        by_head[pos[0] ^ k] = piece[...]
    joined = jnp.concatenate([by_head[h] for h in range(count)], axis=1)
    cols = first[0].shape[0]
    for k in range(count):
        for flip, shard in ((0, first[k]), (1, second[k])):
            at = pl.multiple_of((pos[2] ^ flip) * cols, 16)
            weights[k, pl.ds(at, cols), :] = shard[...]
        total = lax.dot_general(
            joined, weights[k], (((1,), (1,)), ((), ())), preferred_element_type=jnp.float32
        )
        at = pl.multiple_of((pos[0] ^ k) * 2 * cols, 128)
        out[:, pl.ds(at, 2 * cols)] = total.astype(jnp.bfloat16)


def ffn_kernel(parts, pos, mine, theirs, window, taps, glu_own, *refs):
    pieces, w_pw, refs = refs[: 2 * parts], refs[2 * parts], refs[2 * parts + 1 :]
    stream_own, hidden_out, part_out, stream, normed, gated, w_a, w_b, w_c, w_d, sems = refs
    copies = [pltpu.make_async_copy(glu_own, w_a, sems.at[0])]
    for i, piece in enumerate(pieces):
        target, at = (w_b, w_c)[i // parts], (i % parts) * piece.shape[1]
        copies.append(
            pltpu.make_async_copy(
                piece, target.at[:, pl.ds(at, piece.shape[1]), :], sems.at[1 + i]
            )
        )
    copies.append(pltpu.make_async_copy(w_pw, w_d, sems.at[1 + len(pieces)]))
    for copy in copies:
        copy.start()
    wide, _ = window.shape
    rows, half = stream_own.shape
    rim = (wide - rows) // 2
    total = mine[...].astype(jnp.float32) + theirs[...].astype(jnp.float32)
    stream[...] = (window[...].astype(jnp.float32) + total).astype(jnp.bfloat16)
    normed[...] = normalised((stream[...],))[0]
    stream_own[...] = stream[
        rim : rim + rows, pl.ds(pl.multiple_of(pos[3] * half, 128), half)
    ]
    quarter = half // 2
    start = pl.multiple_of(pos[1] * half, 128)
    lhs = [normed[:, pl.ds(start, half)]]
    for flip in range(2):
        start = pl.multiple_of((1 - pos[1]) * half + (pos[2] ^ flip) * quarter, 128)
        lhs.append(normed[:, pl.ds(start, quarter)])
    pre = [0.0, 0.0]
    for j, (cols, w) in enumerate(zip(lhs, (w_a, w_b, w_c))):
        for copy in copies[:1] if j == 0 else copies[1 + (j - 1) * parts : 1 + j * parts]:
            copy.wait()
        pre = [pre[g] + dot(cols, w[g]) for g in range(2)]
    positions = pos[0] * rows - rim + lax.broadcasted_iota(jnp.int32, (wide, 1), 0)
    live = (positions >= 0) & (positions < pos[4])
    product = jnp.where(live, pre[0] * jax.nn.sigmoid(pre[1]), 0.0)
    gated[...] = product.astype(jnp.bfloat16).astype(jnp.float32)
    first = rim - KERNEL // 2
    for lane in range(0, half, 128):
        depth = jnp.zeros((rows, 128), jnp.float32)
        for tap in range(KERNEL):
            depth = depth + gated[first + tap : first + tap + rows, lane : lane + 128] * taps[
                tap : tap + 1, lane : lane + 128
            ].astype(jnp.float32)
        hidden_out[:, lane : lane + 128] = (depth * jax.nn.sigmoid(depth)).astype(jnp.bfloat16)
    copies[-1].wait()
    part_out[...] = dot(hidden_out[...], w_d[...]).astype(jnp.bfloat16)


def pw_kernel(parts, pos, hidden, part_own, *refs):
    pieces, (keep, send) = refs[: 2 * parts], refs[2 * parts :]
    quarter = hidden.shape[1] // 2
    total = 0.0
    for flip in range(2):
        at = pl.multiple_of((pos[2] ^ flip) * quarter, 128)
        cols = hidden[:, pl.ds(at, quarter)]
        size = quarter // parts
        for i in range(parts):
            total = total + dot(cols[:, i * size : (i + 1) * size], pieces[flip * parts + i][...])
    other = total.astype(jnp.bfloat16)
    same = pos[1] == pos[3]
    keep[...] = jnp.where(same, part_own[...], other)
    send[...] = jnp.where(same, other, part_own[...])


def head_shards(frames_in, lengths, w_query, w_key, w_value, w_out, w_glu, dw_kernel, w_pw):
    bf16 = jnp.bfloat16
    blocks = lax.axis_size("frames")
    z = lax.axis_index("frames")
    x = lax.axis_index("fsdp")
    y = lax.axis_index("groups")
    c = lax.axis_index("heads")
    own = frames_in[0]
    rows, half = own.shape
    length = lengths[0]
    rim = 16 * (-(-(KERNEL // 2) // 16))
    wide = rows + 2 * rim
    pos = jnp.stack([z, x, y, c, length]).astype(jnp.int32)

    def shape(*dims):
        return jax.ShapeDtypeStruct(dims, bf16)

    far = swap(own, "frames", 3)
    c_own = swap(own, "heads", 1)
    near = swap(own, "frames", 1)
    relayed = swap(far, "frames", 1)
    c_near = swap(near, "heads", 1)
    c_far = swap(far, "heads", 1)
    c_relayed = swap(relayed, "heads", 1)

    groups = 128 // math.gcd(128, 3 * HEAD_DIM)
    packed = local(
        pack_kernel,
        [shape(w_query.shape[0] // groups, groups * 3 * HEAD_DIM)] * blocks,
        (pos, w_query, w_key, w_value),
    )
    w_mine = [packed[0]] + [swap(packed[k], "frames", k) for k in range(1, blocks)]
    w_other = [swap(w_mine[k], "fsdp", 1) for k in range(blocks)]

    out_own = w_out.T
    out_other = swap(out_own, "fsdp", 1)
    out_send = jnp.where(x == y, out_own, out_other)
    out_keep = jnp.where(x == y, out_other, out_own)
    out_far = swap(out_send, "frames", 3)
    out_near = swap(out_send, "frames", 1)
    out_relayed = swap(out_far, "frames", 1)
    out_first = [out_send, out_near, out_relayed, out_far]
    out_second = [out_keep] + [swap(out_first[k], "groups", 1) for k in range(1, blocks)]

    glu_own = w_glu.transpose(1, 0, 2)
    glu_rows = glu_own.shape[1] // 2
    chunk = glu_rows // GLU_PARTS
    glu_a = [
        swap(lax.dynamic_slice_in_dim(glu_own, y * glu_rows + i * chunk, chunk, 1), "fsdp", 1)
        for i in range(GLU_PARTS)
    ]
    glu_b = [swap(t, "groups", 1) for t in glu_a]
    pw_rows = w_pw.shape[0] // 2
    chunk_pw = pw_rows // PW_PARTS
    pw_a = [
        swap(lax.dynamic_slice_in_dim(w_pw, y * pw_rows + i * chunk_pw, chunk_pw, 0), "fsdp", 1)
        for i in range(PW_PARTS)
    ]
    pw_b = [swap(t, "groups", 1) for t in pw_a]

    w_full, three, window = local(
        functools.partial(early_kernel, blocks),
        [
            shape(2 * blocks * rows, 3 * HEAD_DIM),
            shape(3, rows, 3 * HEAD_DIM),
            shape(wide, 2 * half),
        ],
        (pos, *w_mine, *w_other, own, c_own, near, c_near, far, c_far),
        flops=6 * rows * 2 * half * 3 * HEAD_DIM,
    )
    windows = local(
        attend_kernel,
        [shape(wide, HEAD_DIM)] * blocks,
        (pos, relayed, c_relayed, w_full, three),
        [
            pltpu.VMEM((blocks * rows, 3 * HEAD_DIM), bf16),
            pltpu.VMEM((blocks * rows + 2 * rim, HEAD_DIM), bf16),
        ],
        flops=4 * (blocks * rows) ** 2 * HEAD_DIM,
    )

    heads_in = [windows[0]] + [swap(windows[k], "frames", k) for k in range(1, blocks)]
    partial_value = local(
        out_kernel,
        shape(wide, 2 * half),
        (pos, *heads_in, *out_first, *out_second),
        [
            pltpu.VMEM((blocks, wide, HEAD_DIM), bf16),
            pltpu.VMEM((blocks, 2 * out_own.shape[0], out_own.shape[1]), bf16),
        ],
        flops=2 * wide * blocks * HEAD_DIM * 2 * half,
    )
    partial_other = swap(partial_value, "heads", 1)

    channels = w_glu.shape[2]
    stream_own, hidden, part_own = local(
        functools.partial(ffn_kernel, GLU_PARTS),
        [shape(rows, half), shape(rows, channels), shape(rows, w_pw.shape[1])],
        (pos, partial_value, partial_other, window, dw_kernel, glu_own, *glu_a, *glu_b, w_pw),
        [
            pltpu.VMEM((wide, 2 * half), bf16),
            pltpu.VMEM((wide, 2 * half), bf16),
            pltpu.VMEM((wide, channels), jnp.float32),
            pltpu.VMEM(glu_own.shape, bf16),
            pltpu.VMEM((2, glu_rows, channels), bf16),
            pltpu.VMEM((2, glu_rows, channels), bf16),
            pltpu.VMEM(w_pw.shape, bf16),
            pltpu.SemaphoreType.DMA((2 + 2 * GLU_PARTS,)),
        ],
        flops=8 * wide * half * channels,
        in_place=range(5, 7 + 2 * GLU_PARTS),
    )
    keep, send = local(
        functools.partial(pw_kernel, PW_PARTS),
        [shape(rows, w_pw.shape[1])] * 2,
        (pos, hidden, part_own, *pw_a, *pw_b),
        flops=2 * rows * channels * half,
    )
    arrived = swap(send, "heads", 1)
    conv = keep.astype(jnp.float32) + arrived.astype(jnp.float32)
    return (stream_own.astype(jnp.float32) + conv).astype(bf16)[None]


GLU_PARTS = 2
PW_PARTS = 1


def solution(mesh):
    in_specs = (
        P(("groups", "fsdp"), "frames", "heads"),
        P(("groups", "fsdp")),
        P(("frames", "fsdp"), "heads"),
        P(("frames", "fsdp"), "heads"),
        P(("frames", "fsdp"), "heads"),
        P("heads", ("frames", "fsdp")),
        P("fsdp", None, "heads"),
        P(None, "heads"),
        P("heads", "fsdp"),
    )
    out_specs = P(("groups", "fsdp"), "frames", "heads")
    sizes = mesh.shape
    by_mesh = sizes["frames"] == 4 and sizes["fsdp"] == sizes["groups"] == sizes["heads"] == 2

    def shards(*args):
        if not (by_mesh and args[2].shape[1] == sizes["frames"] * HEAD_DIM):
            return general_shards(*args)
        return head_shards(*args)

    return jax.shard_map(shards, mesh=mesh, in_specs=in_specs, out_specs=out_specs, check_vma=False)
```
